128 devices in a mesh: row: 8 (over y, core), col: 16 (over z, x).
Axes of the slice: x: 4, y: 4, z: 4, core: 2. Of those that a mesh axis runs over, the one named last changes fastest.
Arguments:
- wavefield: bfloat16 [65536, 2, 128], P(('col', 'row')), may hold values from -6 to 6
- recorded: bfloat16 [65536, 2, 128], P(('row', 'col')), may hold values from -6 to 6
- v_bases: bfloat16 [256, 256, 32, 256], P('row', 'col'), may hold values from -0.25 to 0.25
- u_bases: bfloat16 [256, 256, 32, 256], P(('row', 'col')), may hold values from -0.0625 to 0.0625
- ranks: int32 [256, 256], P('row', 'col'), may hold values from 1 to 16
Outputs:
- residual: float32 [65536, 2, 128], P(('row', 'col'))
- gradient: float32 [65536, 2, 128], P(('col', 'row'))
The draws below stay inside these ranges and needn't reach their ends.
Inputs may be any that keep to these rules, and one draw needn't show every extreme that they name: `ranks`: some tile has rank 16.
All inputs are finite; a program needn't handle non-finite values.
Results may differ from the reference program's by a relative error of at most 0.0038.
Values may be sent and summed in bfloat16 or wider, within the bound.
No kernel may reach another device: no remote copies, remote signals or barrier semaphores. Data moves between devices by JAX's collectives and lax.ppermute only.
A program may use at most 128 MiB of HBM per device.

```python
import jax
import jax.numpy as jnp
from jax import lax

TILE = 256
RK = 16
S = 128
NTR = 256
NTC = 256
NREC = 65536
NSRC = 65536


def set_ends(result, rng, smallest, high):
    shape = result.shape
    spot = [jax.random.randint(jax.random.fold_in(rng, axis), (), 0, shape[axis]) for axis in range(len(shape))]
    result = result.at[tuple(spot)].set(smallest)
    longest = shape.index(max(shape))
    spot[longest] = (spot[longest] + 1) % shape[longest]
    return result.at[tuple(spot)].set(high)


def block_scale(key, shape, pieces, least, top_value):
    factor_of = 1.0
    for dim, shards_of in pieces:
        heights = jax.random.uniform(jax.random.fold_in(jax.random.fold_in(key, 6), dim), (shards_of,), jnp.float32, least / len(pieces), top_value / len(pieces))
        factor_of = factor_of * jnp.repeat(jnp.exp(heights), shape[dim] // shards_of).reshape((-1,) + (1,) * (len(shape) - 1 - dim))
    return factor_of


def noise(own_key, dims, scale, bound, split=(), held_as=jnp.bfloat16):
    array = scale * jax.random.normal(own_key, dims, jnp.float32)
    if split:
        array = array * block_scale(own_key, dims, split, -0.22, 0.18)
    return jnp.clip(array, -bound, bound).astype(held_as)


def setup_inputs(seed: int = 0) -> dict:
    key_list = jax.random.split(jax.random.key(seed), 6)
    wavefield = noise(key_list[0], (NSRC, 2, S), 1.0, 6.0, ((0, 128),))
    recorded = noise(key_list[1], (NREC, 2, S), 1.0, 6.0, ((0, 128),))
    v_bases = noise(key_list[2], (NTR, NTC, 2 * RK, TILE), (2 * TILE) ** -0.5, 0.25, ((0, 8), (1, 16)))
    u_bases = noise(key_list[3], (NTR, NTC, 2 * RK, TILE), (2 * RK * NTC) ** -0.5, 0.0625, ((0, 128),))
    ranks = set_ends(jax.random.randint(key_list[4], (NTR, NTC), 1, RK + 1), jax.random.fold_in(key_list[4], 1), 1, RK).astype(jnp.int32)
    return dict(wavefield=wavefield, recorded=recorded, v_bases=v_bases, u_bases=u_bases, ranks=ranks)


def combine_adjoint(prod):
    half = prod.shape[2] // 2
    real = prod[:, :, :half, 0] + prod[:, :, half:, 1]
    imag = prod[:, :, :half, 1] - prod[:, :, half:, 0]
    return jnp.stack([real, imag], axis=3)


def stacked(coeffs):
    real = coeffs[:, :, :, 0]
    imag = coeffs[:, :, :, 1]
    first = jnp.concatenate([real, -imag], axis=2)
    second = jnp.concatenate([imag, real], axis=2)
    return jnp.stack([first, second], axis=3)


def reference(wavefield, recorded, v_bases, u_bases, ranks):
    blocks = wavefield.astype(jnp.float32).reshape(NTC, TILE, 2, S)
    levels = lax.broadcasted_iota(jnp.int32, (NTR, NTC, RK), 2)
    mask = (levels < ranks[:, :, None]).astype(jnp.float32)
    rows = recorded.reshape(NTR, TILE, 2, S)

    def step(total, item):
        v_row, u_row, m_row, d_row = item
        v_row = v_row[None].astype(jnp.float32)
        u_row = u_row[None].astype(jnp.float32)
        m_row = m_row[None]
        prod = jnp.einsum("ijrk,jkcs->ijrcs", v_row, blocks)
        coeffs = (combine_adjoint(prod) * m_row[:, :, :, None, None]).astype(jnp.bfloat16)
        modelled = jnp.einsum("ijrk,ijrcs->ikcs", u_row, stacked(coeffs.astype(jnp.float32)))[0]
        res_row = modelled - d_row.astype(jnp.float32)
        rounded = res_row.astype(jnp.bfloat16).astype(jnp.float32)
        prod_back = jnp.einsum("ijrk,ikcs->ijrcs", u_row, rounded[None])
        back = combine_adjoint(prod_back).astype(jnp.bfloat16).astype(jnp.float32)
        back = back * m_row[:, :, :, None, None]
        total = total + jnp.einsum("ijrk,ijrcs->jkcs", v_row, stacked(back))
        return total, res_row

    start = jnp.zeros((NTC, TILE, 2, S), jnp.float32)
    total, res_rows = lax.scan(step, start, (v_bases, u_bases, mask, rows))
    return res_rows.reshape(NREC, 2, S), total.reshape(NSRC, 2, S)
```

```python
import functools

import jax
import jax.numpy as jnp
from jax import lax
from jax.experimental import pallas as pl
from jax.experimental.pallas import tpu as pltpu
from jax.sharding import PartitionSpec as P

F32 = jnp.float32
BF16 = jnp.bfloat16


def dot(a, b):
    return jnp.dot(a, b, preferred_element_type=F32)


def v_adjoint_kernel(pos, ranks, same, other, v, out):
    tiles, _, twice, tile = v.shape
    rank = twice // 2
    half = same.shape[3] // 2
    ncol = 4 * pl.num_programs(0)
    first = 4 * lax.rem(pos[0] + pl.program_id(0), pl.num_programs(0))
    level = lax.broadcasted_iota(jnp.int32, (rank, 2 * half), 0)
    for held, core in ((same, pos[1]), (other, 1 - pos[1])):
        for t in range(2):
            j = core * 2 + t
            x = held[0, t]
            turned = jnp.concatenate([x[:, half:], -x[:, :half]], axis=1)
            real = v[:, j, :rank, :].reshape(tiles * rank, tile)
            imag = v[:, j, rank:, :].reshape(tiles * rank, tile)
            prod = dot(real, x) + dot(imag, turned)
            for i in range(tiles):
                keep = level < ranks[i * ncol + first + j]
                piece = prod[i * rank : (i + 1) * rank]
                out[i, j] = jnp.where(keep, piece, 0.0).astype(BF16)


def v_adjoint(pos, ranks, same, other, v):
    tiles, ncol, twice, tile = v.shape
    chips, _, _, wide = same.shape
    spot = lambda d, pos, ranks: (0, lax.rem(pos[0] + d, chips), 0, 0)
    near = lambda d, pos, ranks: (d, 0, 0, 0)
    return pl.pallas_call(
        v_adjoint_kernel,
        out_shape=jax.ShapeDtypeStruct((tiles, ncol, twice // 2, wide), BF16),
        grid_spec=pltpu.PrefetchScalarGridSpec(
            num_scalar_prefetch=2,
            grid=(chips,),
            in_specs=[
                pl.BlockSpec((1, 2, tile, wide), near),
                pl.BlockSpec((1, 2, tile, wide), near),
                pl.BlockSpec((tiles, 4, twice, tile), spot),
            ],
            out_specs=pl.BlockSpec((tiles, 4, twice // 2, wide), spot),
        ),
        compiler_params=pltpu.CompilerParams(vmem_limit_bytes=48 << 20),
        name="v_adjoint",
    )(pos, ranks, same, other, v)


def u_both_kernel(coeffs, u, recorded, residual, back):
    sources, _, cols, rank, wide = coeffs.shape
    half = wide // 2
    tile = u.shape[3]
    total = jnp.zeros((wide, tile), F32)
    for s in range(sources):
        c = coeffs[s, 0].reshape(cols * rank, wide).T
        turned = jnp.concatenate([-c[half:], c[:half]], axis=0)
        real = u[0, s * cols : (s + 1) * cols, :rank, :].reshape(cols * rank, tile)
        imag = u[0, s * cols : (s + 1) * cols, rank:, :].reshape(cols * rank, tile)
        total = total + dot(c, real) + dot(turned, imag)
    res = total.T - recorded[...].astype(F32)
    residual[...] = res
    r = res.astype(BF16)
    turned = jnp.concatenate([r[:, half:], -r[:, :half]], axis=1)
    for s in range(sources):
        real = u[0, s * cols : (s + 1) * cols, :rank, :].reshape(cols * rank, tile)
        imag = u[0, s * cols : (s + 1) * cols, rank:, :].reshape(cols * rank, tile)
        prod = dot(real, r) + dot(imag, turned)
        back[s, 0] = prod.astype(BF16).reshape(cols, rank, wide)


def u_both(coeffs, u, recorded):
    sources, rows, cols, rank, wide = coeffs.shape
    _, ncol, twice, tile = u.shape
    piece = pl.BlockSpec((sources, 1, cols, rank, wide), lambda i: (0, i, 0, 0, 0))
    flat = pl.BlockSpec((tile, wide), lambda i: (i, 0))
    return pl.pallas_call(
        u_both_kernel,
        out_shape=(
            jax.ShapeDtypeStruct((rows * tile, wide), F32),
            jax.ShapeDtypeStruct(coeffs.shape, BF16),
        ),
        grid=(rows,),
        in_specs=[piece, pl.BlockSpec((1, ncol, twice, tile), lambda i: (i, 0, 0, 0)), flat],
        out_specs=(flat, piece),
        compiler_params=pltpu.CompilerParams(vmem_limit_bytes=48 << 20),
        name="u_both",
    )(coeffs, u, recorded)


def v_apply_kernel(pos, ranks, back, v, own, partner):
    tiles, _, twice, tile = v.shape
    rank = twice // 2
    wide = back.shape[3]
    half = wide // 2
    ncol = 4 * pl.num_programs(0)
    first = 4 * lax.rem(pos[0] + pl.program_id(0), pl.num_programs(0))
    level = lax.broadcasted_iota(jnp.int32, (rank, wide), 0)
    for goes, core in ((partner, 1 - pos[1]), (own, pos[1])):
        for t in range(2):
            j = core * 2 + t
            rows = []
            for i in range(tiles):
                keep = level < ranks[i * ncol + first + j]
                rows.append(jnp.where(keep, back[i, j].astype(F32), 0.0))
            b = jnp.concatenate(rows, axis=0).astype(BF16).T
            turned = jnp.concatenate([-b[half:], b[:half]], axis=0)
            real = v[:, j, :rank, :].reshape(tiles * rank, tile)
            imag = v[:, j, rank:, :].reshape(tiles * rank, tile)
            goes[0, t] = (dot(b, real) + dot(turned, imag)).astype(goes.dtype)


def v_apply(pos, ranks, back, v):
    tiles, ncol, twice, tile = v.shape
    wide = back.shape[3]
    chips = ncol // 4
    spot = lambda d, pos, ranks: (0, lax.rem(pos[0] + d, chips), 0, 0)
    near = lambda d, pos, ranks: (d, 0, 0, 0)
    return pl.pallas_call(
        v_apply_kernel,
        out_shape=(
            jax.ShapeDtypeStruct((chips, 2, wide, tile), F32),
            jax.ShapeDtypeStruct((chips, 2, wide, tile), BF16),
        ),
        grid_spec=pltpu.PrefetchScalarGridSpec(
            num_scalar_prefetch=2,
            grid=(chips,),
            in_specs=[
                pl.BlockSpec((tiles, 4, twice // 2, wide), spot),
                pl.BlockSpec((tiles, 4, twice, tile), spot),
            ],
            out_specs=(
                pl.BlockSpec((1, 2, wide, tile), near),
                pl.BlockSpec((1, 2, wide, tile), near),
            ),
        ),
        compiler_params=pltpu.CompilerParams(vmem_limit_bytes=48 << 20),
        name="v_apply",
    )(pos, ranks, back, v)


def body(chips, wavefield, recorded, v_bases, u_bases, ranks):
    tile = v_bases.shape[3]
    wide = 2 * wavefield.shape[2]
    me = lax.axis_index("row")
    pos = jnp.stack([me // 2, me % 2]).astype(jnp.int32)
    flat_ranks = ranks.reshape(-1)
    swap = [(r, r ^ 1) for r in range(2 * chips)]

    def hop(d):
        return [(r, (r + 2 * d) % (2 * chips)) for r in range(2 * chips)]

    mine = wavefield.reshape(-1, tile, wide)
    along = [mine] + [lax.ppermute(mine, "row", hop(chips - d)) for d in range(1, chips)]
    same = jnp.stack(along)
    other = lax.ppermute(same, "row", swap)
    coeffs = v_adjoint(pos, flat_ranks, same, other, v_bases)

    moved = lax.all_to_all(coeffs, "col", split_axis=0, concat_axis=0, tiled=True)
    rows = u_bases.shape[0]
    cols, rank = coeffs.shape[1], coeffs.shape[2]
    moved = moved.reshape(-1, rows, cols, rank, wide)
    residual, back = u_both(moved, u_bases, recorded.reshape(-1, wide))
    back = back.reshape(-1, cols, rank, wide)
    back = lax.all_to_all(back, "col", split_axis=0, concat_axis=0, tiled=True)

    own, partner = v_apply(pos, flat_ranks, back, v_bases)
    met = own + lax.ppermute(partner, "row", swap).astype(F32)
    total = met[0]
    for d in range(1, chips):
        total = total + lax.ppermute(met[d].astype(BF16), "row", hop(d)).astype(F32)
    gradient = total.reshape(2, 2, wide // 2, tile).transpose(0, 3, 1, 2)
    return residual.reshape(recorded.shape), gradient.reshape(wavefield.shape)


def solution(mesh):
    in_specs = (
        P(("col", "row"), None, None),
        P(("row", "col"), None, None),
        P("row", "col", None, None),
        P(("row", "col"), None, None, None),
        P("row", "col"),
    )
    out_specs = (P(("row", "col"), None, None), P(("col", "row"), None, None))
    step = functools.partial(body, mesh.shape["row"] // 2)
    return jax.shard_map(step, mesh=mesh, in_specs=in_specs, out_specs=out_specs, check_vma=False)
```

```python
import functools

import jax
import jax.numpy as jnp
from jax import lax
from jax.experimental import pallas as pl
from jax.experimental.pallas import tpu as pltpu
from jax.sharding import PartitionSpec as P

F32 = jnp.float32
BF16 = jnp.bfloat16
INSIDE = pl.BlockSpec(memory_space=pltpu.VMEM)
SCALAR = pl.BlockSpec(memory_space=pltpu.SMEM)


SMALL = pltpu.CompilerParams(vmem_limit_bytes=12 << 20)


def dot(a, b):
    return jnp.dot(a, b, preferred_element_type=F32)


def cost(flops, moved):
    return pl.CostEstimate(flops=flops, bytes_accessed=moved, transcendentals=0)


def v_adjoint_kernel(count, pairs, ranks, x, v, *rest):
    out, held, sems = rest[-3:]
    _, tiles, _, twice, tile = held.shape
    ncol = out.shape[1]
    rank = twice // 2
    wide = x.shape[2]
    half = wide // 2
    level = lax.broadcasted_iota(jnp.int32, (rank, wide), 0)
    copies = [
        pltpu.make_async_copy(v.at[:, pl.ds(pairs[n] * 2, 2)], held.at[n], sems.at[n])
        for n in range(count)
    ]
    for copy in copies:
        copy.start()
    for n in range(count):
        copies[n].wait()
        for t in range(2):
            j = pairs[n] * 2 + t
            block = x[n * 2 + t]
            turned = jnp.concatenate([block[:, half:], -block[:, :half]], axis=1)
            real = held[n, :, t, :rank, :].reshape(tiles * rank, tile)
            imag = held[n, :, t, rank:, :].reshape(tiles * rank, tile)
            prod = dot(real, block) + dot(imag, turned)
            for i in range(tiles):
                keep = level < ranks[i * ncol + j]
                piece = prod[i * rank : (i + 1) * rank]
                out[i, j] = jnp.where(keep, piece, 0.0).astype(BF16)


def v_adjoint(pairs, ranks, x, v, held):
    tiles, ncol, twice, tile = v.shape
    blocks, _, wide = x.shape
    count = blocks // 2
    more = () if held is None else (held,)
    return pl.pallas_call(
        functools.partial(v_adjoint_kernel, count),
        out_shape=jax.ShapeDtypeStruct((tiles, ncol, twice // 2, wide), BF16),
        in_specs=[SCALAR, SCALAR, INSIDE, pl.BlockSpec(memory_space=pltpu.HBM)]
        + [INSIDE] * len(more),
        out_specs=INSIDE,
        scratch_shapes=[
            pltpu.VMEM((count, tiles, 2, twice, tile), BF16),
            pltpu.SemaphoreType.DMA((count,)),
        ],
        input_output_aliases={4: 0} if more else {},
        cost_estimate=cost(2 * blocks * tiles * twice * tile * wide, blocks * tiles * twice * tile * 2),
        compiler_params=SMALL,
        name="v_adjoint",
    )(pairs, ranks, x, v, *more)


def u_both_kernel(coeffs, u, recorded, residual, back):
    sources, rows, cols, rank, wide = coeffs.shape
    half = wide // 2
    tile = u.shape[3]

    def bases(i, s):
        real = u[i, s * cols : (s + 1) * cols, :rank, :].reshape(cols * rank, tile)
        imag = u[i, s * cols : (s + 1) * cols, rank:, :].reshape(cols * rank, tile)
        return real, imag

    for i in range(rows):
        total = jnp.zeros((wide, tile), F32)
        for s in range(sources):
            c = coeffs[s, i].reshape(cols * rank, wide).T
            turned = jnp.concatenate([-c[half:], c[:half]], axis=0)
            real, imag = bases(i, s)
            total = total + dot(c, real) + dot(turned, imag)
        res = total.T - recorded[i * tile : (i + 1) * tile, :].astype(F32)
        residual[i * tile : (i + 1) * tile, :] = res
        r = res.astype(BF16)
        turned = jnp.concatenate([r[:, half:], -r[:, :half]], axis=1)
        for s in range(sources):
            real, imag = bases(i, s)
            prod = dot(real, r) + dot(imag, turned)
            back[s, i] = prod.astype(BF16).reshape(cols, rank, wide)


def u_both(coeffs, u, recorded):
    rows, _, _, tile = u.shape
    wide = coeffs.shape[4]
    return pl.pallas_call(
        u_both_kernel,
        out_shape=(
            jax.ShapeDtypeStruct((rows * tile, wide), F32),
            jax.ShapeDtypeStruct(coeffs.shape, BF16),
        ),
        in_specs=[INSIDE] * 3,
        out_specs=(INSIDE, INSIDE),
        cost_estimate=cost(4 * u.size * wide, 2 * u.size),
        compiler_params=SMALL,
        name="u_both",
    )(coeffs, u, recorded)


def v_apply_kernel(blocks, pairs, ranks, back, v, out):
    tiles, ncol, twice, tile = v.shape
    rank = twice // 2
    wide = back.shape[3]
    half = wide // 2
    level = lax.broadcasted_iota(jnp.int32, (rank, wide), 0)
    for n in range(blocks):
        j = pairs[n // 2] * 2 + n % 2
        rows = []
        for i in range(tiles):
            keep = level < ranks[i * ncol + j]
            rows.append(jnp.where(keep, back[i, j].astype(F32), 0.0))
        b = jnp.concatenate(rows, axis=0).astype(BF16).T
        turned = jnp.concatenate([-b[half:], b[:half]], axis=0)
        real = v[:, j, :rank, :].reshape(tiles * rank, tile)
        imag = v[:, j, rank:, :].reshape(tiles * rank, tile)
        out[n] = (dot(b, real) + dot(turned, imag)).astype(out.dtype)


def v_apply(pairs, ranks, back, v, dtype):
    tiles, ncol, twice, tile = v.shape
    wide = back.shape[3]
    blocks = ncol // 2
    return pl.pallas_call(
        functools.partial(v_apply_kernel, blocks),
        out_shape=jax.ShapeDtypeStruct((blocks, wide, tile), dtype),
        in_specs=[SCALAR, SCALAR, INSIDE, INSIDE],
        out_specs=INSIDE,
        cost_estimate=cost(2 * blocks * tiles * twice * tile * wide, blocks * tiles * twice * tile * 2),
        compiler_params=SMALL,
        name="v_apply",
    )(pairs, ranks, back, v)


def body(chips, wavefield, recorded, v_bases, u_bases, ranks):
    tile = v_bases.shape[3]
    wide = 2 * wavefield.shape[2]
    me = lax.axis_index("row")
    y, core = me // 2, me % 2
    flat_ranks = ranks.reshape(-1)
    swap = [(r, r ^ 1) for r in range(2 * chips)]

    def hop(d):
        return [(r, (r + 2 * d) % (2 * chips)) for r in range(2 * chips)]

    whole = jnp.arange(chips)

    def pairs(core):
        return (y + whole) % chips * 2 + core

    mine = wavefield.reshape(-1, tile, wide)
    v_outside = pltpu.with_memory_space_constraint(v_bases, pltpu.HBM)
    same = [mine] + [lax.ppermute(mine, "row", hop(chips - d)) for d in range(1, chips)]
    same = jnp.concatenate(same)
    other = lax.ppermute(same, "row", swap)
    near, far = pairs(core), pairs(1 - core)
    coeffs = v_adjoint(near, flat_ranks, same, v_outside, None)
    coeffs = v_adjoint(far, flat_ranks, other, v_outside, coeffs)

    data = recorded.reshape(-1, wide)
    coeffs, data, near, far = lax.optimization_barrier((coeffs, data, near, far))
    moved = lax.all_to_all(coeffs, "col", split_axis=0, concat_axis=0, tiled=True)
    ncol, rank = coeffs.shape[1], coeffs.shape[2]
    moved = moved.reshape(-1, u_bases.shape[0], ncol, rank, wide)
    residual, back = u_both(moved, u_bases, data)
    back = back.reshape(-1, ncol, rank, wide)
    back = lax.all_to_all(back, "col", split_axis=0, concat_axis=0, tiled=True)

    theirs = v_apply(far, flat_ranks, back, v_bases, BF16)
    theirs = lax.ppermute(theirs, "row", swap)
    own = v_apply(near, flat_ranks, back, v_bases, F32)
    met = (own + theirs.astype(F32)).reshape(chips, 2, wide, tile)
    total = met[0]
    for d in (2, 1, 3):
        total = total + lax.ppermute(met[d].astype(BF16), "row", hop(d)).astype(F32)
    gradient = total.reshape(2, 2, wide // 2, tile).transpose(0, 3, 1, 2)
    return residual.reshape(recorded.shape), gradient.reshape(wavefield.shape)


def solution(mesh):
    in_specs = (
        P(("col", "row"), None, None),
        P(("row", "col"), None, None),
        P("row", "col", None, None),
        P(("row", "col"), None, None, None),
        P("row", "col"),
    )
    out_specs = (P(("row", "col"), None, None), P(("col", "row"), None, None))
    step = functools.partial(body, mesh.shape["row"] // 2)
    return jax.shard_map(step, mesh=mesh, in_specs=in_specs, out_specs=out_specs, check_vma=False)
```

```python
import functools

import jax
import jax.numpy as jnp
from jax import lax
from jax.experimental import pallas as pl
from jax.experimental.pallas import tpu as pltpu
from jax.sharding import PartitionSpec as P

F32 = jnp.float32
BF16 = jnp.bfloat16
INSIDE = pl.BlockSpec(memory_space=pltpu.VMEM)
SCALAR = pl.BlockSpec(memory_space=pltpu.SMEM)


LAG = 22000
SMALL = pltpu.CompilerParams(vmem_limit_bytes=12 << 20)


def dot(a, b):
    return jnp.dot(a, b, preferred_element_type=F32)


def cost(flops, moved):
    return pl.CostEstimate(flops=flops, bytes_accessed=moved, transcendentals=0)


def v_adjoint_kernel(away, lag, pairs, ranks, x, v, *rest):
    out, mark = rest[-2:]
    tiles, ncol, twice, tile = v.shape
    rank = twice // 2
    wide = x.shape[2]
    half = wide // 2
    level = lax.broadcasted_iota(jnp.int32, (rank, wide), 0)
    for t in range(2):
        j = pairs[away] * 2 + t
        block = x[t]
        turned = jnp.concatenate([block[:, half:], -block[:, :half]], axis=1)
        real = v[:, j, :rank, :].reshape(tiles * rank, tile)
        imag = v[:, j, rank:, :].reshape(tiles * rank, tile)
        prod = dot(real, block) + dot(imag, turned)
        for i in range(tiles):
            keep = level < ranks[i * ncol + j]
            piece = prod[i * rank : (i + 1) * rank]
            out[i, j] = jnp.where(keep, piece, 0.0).astype(BF16)
    mark[...] = jnp.zeros_like(mark)
    if lag:
        pl.when(lax.rem(pairs[0], 2) == 0)(lambda: pl.delay(lag))


def v_adjoint(pairs, away, ranks, x, v, held, lag=0):
    tiles, ncol, twice, tile = v.shape
    blocks, _, wide = x.shape
    more = () if held is None else (held,)
    return pl.pallas_call(
        functools.partial(v_adjoint_kernel, away, lag),
        out_shape=(
            jax.ShapeDtypeStruct((tiles, ncol, twice // 2, wide), BF16),
            jax.ShapeDtypeStruct((8, 128), jnp.int32),
        ),
        in_specs=[SCALAR, SCALAR, INSIDE, INSIDE] + [INSIDE] * len(more),
        out_specs=(INSIDE, INSIDE),
        input_output_aliases={4: 0} if more else {},
        cost_estimate=cost(2 * blocks * tiles * twice * tile * wide, blocks * tiles * twice * tile * 2),
        compiler_params=SMALL,
        name="v_adjoint",
    )(pairs, ranks, x, v, *more)


def u_both_kernel(coeffs, u, recorded, residual, back):
    sources, rows, cols, rank, wide = coeffs.shape
    half = wide // 2
    tile = u.shape[3]

    def bases(i, s):
        real = u[i, s * cols : (s + 1) * cols, :rank, :].reshape(cols * rank, tile)
        imag = u[i, s * cols : (s + 1) * cols, rank:, :].reshape(cols * rank, tile)
        return real, imag

    for i in range(rows):
        total = jnp.zeros((wide, tile), F32)
        for s in range(sources):
            c = coeffs[s, i].reshape(cols * rank, wide).T
            turned = jnp.concatenate([-c[half:], c[:half]], axis=0)
            real, imag = bases(i, s)
            total = total + dot(c, real) + dot(turned, imag)
        res = total.T - recorded[i * tile : (i + 1) * tile, :].astype(F32)
        residual[i * tile : (i + 1) * tile, :] = res
        r = res.astype(BF16)
        turned = jnp.concatenate([r[:, half:], -r[:, :half]], axis=1)
        for s in range(sources):
            real, imag = bases(i, s)
            prod = dot(real, r) + dot(imag, turned)
            back[s, i] = prod.astype(BF16).reshape(cols, rank, wide)


def u_both(coeffs, u, recorded):
    rows, _, _, tile = u.shape
    wide = coeffs.shape[4]
    return pl.pallas_call(
        u_both_kernel,
        out_shape=(
            jax.ShapeDtypeStruct((rows * tile, wide), F32),
            jax.ShapeDtypeStruct(coeffs.shape, BF16),
        ),
        in_specs=[INSIDE] * 3,
        out_specs=(INSIDE, INSIDE),
        cost_estimate=cost(4 * u.size * wide, 2 * u.size),
        compiler_params=SMALL,
        name="u_both",
    )(coeffs, u, recorded)


def v_apply_kernel(blocks, pairs, ranks, back, v, out):
    tiles, ncol, twice, tile = v.shape
    rank = twice // 2
    wide = back.shape[3]
    half = wide // 2
    level = lax.broadcasted_iota(jnp.int32, (rank, wide), 0)
    for n in range(blocks):
        j = pairs[n // 2] * 2 + n % 2
        rows = []
        for i in range(tiles):
            keep = level < ranks[i * ncol + j]
            rows.append(jnp.where(keep, back[i, j].astype(F32), 0.0))
        b = jnp.concatenate(rows, axis=0).astype(BF16).T
        turned = jnp.concatenate([-b[half:], b[:half]], axis=0)
        real = v[:, j, :rank, :].reshape(tiles * rank, tile)
        imag = v[:, j, rank:, :].reshape(tiles * rank, tile)
        out[n] = (dot(b, real) + dot(turned, imag)).astype(out.dtype)


def v_apply(pairs, ranks, back, v, dtype):
    tiles, ncol, twice, tile = v.shape
    wide = back.shape[3]
    blocks = ncol // 2
    return pl.pallas_call(
        functools.partial(v_apply_kernel, blocks),
        out_shape=jax.ShapeDtypeStruct((blocks, wide, tile), dtype),
        in_specs=[SCALAR, SCALAR, INSIDE, INSIDE],
        out_specs=INSIDE,
        cost_estimate=cost(2 * blocks * tiles * twice * tile * wide, blocks * tiles * twice * tile * 2),
        compiler_params=SMALL,
        name="v_apply",
    )(pairs, ranks, back, v)


def body(chips, wavefield, recorded, v_bases, u_bases, ranks):
    tile = v_bases.shape[3]
    wide = 2 * wavefield.shape[2]
    me = lax.axis_index("row")
    y, core = me // 2, me % 2
    flat_ranks = ranks.reshape(-1)
    swap = [(r, r ^ 1) for r in range(2 * chips)]

    def hop(d):
        return [(r, (r + 2 * d) % (2 * chips)) for r in range(2 * chips)]

    whole = jnp.arange(chips)

    def pairs(core):
        return (y + whole) % chips * 2 + core

    mine = wavefield.reshape(-1, tile, wide)
    others = [lax.ppermute(mine, "row", swap)]
    along = [lax.ppermute(mine, "row", hop(chips - d)) for d in range(1, chips)]
    data = recorded.reshape(-1, wide)
    near, far = pairs(core), pairs(1 - core)
    coeffs, _ = v_adjoint(near, 0, flat_ranks, mine, v_bases, None)
    coeffs, mark = v_adjoint(far, 0, flat_ranks, others[0], v_bases, coeffs)
    mark, data, near, far, flat_ranks = lax.optimization_barrier(
        (mark, data, near, far, flat_ranks)
    )
    near = near + mark[0, :chips]
    along = [mine] + [lax.optimization_barrier((part, near))[0] for part in along]
    others += [lax.ppermute(part, "row", swap) for part in along[1:]]
    order = ((near, along, 1), (near, along, 3), (far, others, 1), (far, others, 3), (near, along, 2))
    for numbers, held, d in order:
        coeffs, _ = v_adjoint(numbers, d, flat_ranks, held[d], v_bases, coeffs)
    coeffs, _ = v_adjoint(far, 2, flat_ranks, others[2], v_bases, coeffs, LAG)

    moved = lax.all_to_all(coeffs, "col", split_axis=0, concat_axis=0, tiled=True)
    ncol, rank = coeffs.shape[1], coeffs.shape[2]
    moved = moved.reshape(-1, u_bases.shape[0], ncol, rank, wide)
    residual, back = u_both(moved, u_bases, data)
    back = back.reshape(-1, ncol, rank, wide)
    back = lax.all_to_all(back, "col", split_axis=0, concat_axis=0, tiled=True)

    theirs = v_apply(far, flat_ranks, back, v_bases, BF16)
    theirs = lax.ppermute(theirs, "row", swap)
    own = v_apply(near, flat_ranks, back, v_bases, F32)
    met = (own + theirs.astype(F32)).reshape(chips, 2, wide, tile)
    total = met[0]
    for d in (2, 1, 3):
        total = total + lax.ppermute(met[d].astype(BF16), "row", hop(d)).astype(F32)
    gradient = total.reshape(2, 2, wide // 2, tile).transpose(0, 3, 1, 2)
    return residual.reshape(recorded.shape), gradient.reshape(wavefield.shape)


def solution(mesh):
    in_specs = (
        P(("col", "row"), None, None),
        P(("row", "col"), None, None),
        P("row", "col", None, None),
        P(("row", "col"), None, None, None),
        P("row", "col"),
    )
    out_specs = (P(("row", "col"), None, None), P(("col", "row"), None, None))
    step = functools.partial(body, mesh.shape["row"] // 2)
    return jax.shard_map(step, mesh=mesh, in_specs=in_specs, out_specs=out_specs, check_vma=False)
```

```python
import functools

import jax
import jax.numpy as jnp
from jax import lax
from jax.experimental import pallas as pl
from jax.experimental.pallas import tpu as pltpu
from jax.sharding import PartitionSpec as P

F32 = jnp.float32
BF16 = jnp.bfloat16
INSIDE = pl.BlockSpec(memory_space=pltpu.VMEM)


LAG = 22000
SMALL = pltpu.CompilerParams(vmem_limit_bytes=12 << 20)


def dot(a, b):
    return jnp.dot(a, b, preferred_element_type=F32)


def cost(flops, moved):
    return pl.CostEstimate(flops=flops, bytes_accessed=moved, transcendentals=0)


def column(away, flip, t, chips):
    me = lax.axis_index("row")
    core = lax.rem(me, 2)
    core = 1 - core if flip else core
    return lax.rem(lax.div(me, 2) + away, chips) * 4 + core * 2 + t


def v_adjoint_kernel(items, lag, ranks, v, *rest):
    out, mark = rest[-2:]
    tiles, ncol, twice, tile = v.shape
    rank = twice // 2
    half = ranks.shape[2]
    level = lax.broadcasted_iota(jnp.int32, (rank, half), 0)
    for (away, flip), x in zip(items, rest):
        for t in range(2):
            j = column(away, flip, t, ncol // 4)
            block = x[t]
            turned = jnp.concatenate([block[:, half:], -block[:, :half]], axis=1)
            real = v[:, j, :rank, :].reshape(tiles * rank, tile)
            imag = v[:, j, rank:, :].reshape(tiles * rank, tile)
            prod = dot(real, block) + dot(imag, turned)
            for i in range(tiles):
                keep = level < ranks[j, i : i + 1, :]
                piece = prod[i * rank : (i + 1) * rank]
                for part in (slice(0, half), slice(half, 2 * half)):
                    out[i, j, :, part] = jnp.where(keep, piece[:, part], 0.0).astype(BF16)
    mark[...] = jnp.zeros_like(mark)
    if lag:
        pl.when(lax.rem(lax.axis_index("row"), 2) == 1)(lambda: pl.delay(lag))


def v_adjoint(ranks, v, items, xs, held=None, lag=0):
    tiles, ncol, twice, tile = v.shape
    wide = xs[0].shape[2]
    more = () if held is None else (held,)
    work = 2 * len(xs) * tiles * twice * tile
    return pl.pallas_call(
        functools.partial(v_adjoint_kernel, items, lag),
        out_shape=(
            jax.ShapeDtypeStruct((tiles, ncol, twice // 2, wide), BF16),
            jax.ShapeDtypeStruct((8, 128), jnp.int32),
        ),
        in_specs=[INSIDE] * (2 + len(xs) + len(more)),
        out_specs=(INSIDE, INSIDE),
        input_output_aliases={2 + len(xs): 0} if more else {},
        cost_estimate=cost(2 * work * wide, 2 * work),
        compiler_params=SMALL,
        name="v_adjoint",
    )(ranks, v, *xs, *more)


def u_both_kernel(coeffs, u, recorded, residual, back):
    sources, rows, cols, rank, wide = coeffs.shape
    half = wide // 2
    tile = u.shape[3]

    def bases(i, s):
        real = u[i, s * cols : (s + 1) * cols, :rank, :].reshape(cols * rank, tile)
        imag = u[i, s * cols : (s + 1) * cols, rank:, :].reshape(cols * rank, tile)
        return real, imag

    for i in range(rows):
        total = jnp.zeros((wide, tile), F32)
        for s in range(sources):
            c = coeffs[s, i].reshape(cols * rank, wide).T
            turned = jnp.concatenate([-c[half:], c[:half]], axis=0)
            real, imag = bases(i, s)
            total = total + dot(c, real) + dot(turned, imag)
        res = total.T - recorded[i * tile : (i + 1) * tile, :].astype(F32)
        residual[i * tile : (i + 1) * tile, :] = res
        r = res.astype(BF16)
        turned = jnp.concatenate([r[:, half:], -r[:, :half]], axis=1)
        for s in range(sources):
            real, imag = bases(i, s)
            prod = dot(real, r) + dot(imag, turned)
            back[s, i] = prod.astype(BF16).reshape(cols, rank, wide)


def u_both(coeffs, u, recorded):
    rows, _, _, tile = u.shape
    wide = coeffs.shape[4]
    return pl.pallas_call(
        u_both_kernel,
        out_shape=(
            jax.ShapeDtypeStruct((rows * tile, wide), F32),
            jax.ShapeDtypeStruct(coeffs.shape, BF16),
        ),
        in_specs=[INSIDE] * 3,
        out_specs=(INSIDE, INSIDE),
        cost_estimate=cost(4 * u.size * wide, 2 * u.size),
        compiler_params=SMALL,
        name="u_both",
    )(coeffs, u, recorded)


def v_apply_kernel(flip, ranks, back, v, out):
    tiles, ncol, twice, tile = v.shape
    rank = twice // 2
    half = back.shape[3] // 2
    level = lax.broadcasted_iota(jnp.int32, (rank, 2 * half), 0)
    for n in range(out.shape[0]):
        j = column(n // 2, flip, n % 2, ncol // 4)
        rows = []
        for i in range(tiles):
            top = jnp.concatenate([ranks[j, i : i + 1, :]] * 2, axis=1)
            rows.append(jnp.where(level < top, back[i, j].astype(F32), 0.0))
        b = jnp.concatenate(rows, axis=0).astype(BF16).T
        turned = jnp.concatenate([-b[half:], b[:half]], axis=0)
        real = v[:, j, :rank, :].reshape(tiles * rank, tile)
        imag = v[:, j, rank:, :].reshape(tiles * rank, tile)
        out[n] = (dot(b, real) + dot(turned, imag)).astype(out.dtype)


def v_apply(ranks, back, v, flip, dtype):
    tiles, ncol, twice, tile = v.shape
    wide = back.shape[3]
    blocks = ncol // 2
    return pl.pallas_call(
        functools.partial(v_apply_kernel, flip),
        out_shape=jax.ShapeDtypeStruct((blocks, wide, tile), dtype),
        in_specs=[INSIDE] * 3,
        out_specs=INSIDE,
        cost_estimate=cost(2 * blocks * tiles * twice * tile * wide, blocks * tiles * twice * tile * 2),
        compiler_params=SMALL,
        name="v_apply",
    )(ranks, back, v)


def body(chips, wavefield, recorded, v_bases, u_bases, ranks):
    tile = v_bases.shape[3]
    wide = 2 * wavefield.shape[2]
    swap = [(r, r ^ 1) for r in range(2 * chips)]
    away = range(1, chips)

    def hop(d):
        return [(r, (r + 2 * d) % (2 * chips)) for r in range(2 * chips)]

    mine = wavefield.reshape(-1, tile, wide)
    partner = lax.ppermute(mine, "row", swap)
    along = [lax.ppermute(mine, "row", hop(chips - d)) for d in away]
    tops = jnp.broadcast_to(ranks.T[:, :, None], ranks.shape[::-1] + (wide // 2,))
    data = recorded.reshape(-1, wide)
    coeffs, mark = v_adjoint(tops, v_bases, [(0, 0), (0, 1)], [mine, partner])
    mark, data = lax.optimization_barrier((mark, data))
    along = [lax.optimization_barrier((part, mark))[0] for part in along]
    others = [lax.ppermute(part, "row", swap) for part in along]
    coeffs, _ = v_adjoint(tops, v_bases, [(d, 0) for d in away], along, coeffs)
    coeffs, _ = v_adjoint(tops, v_bases, [(d, 1) for d in away], others, coeffs, LAG)

    moved = lax.all_to_all(coeffs, "col", split_axis=0, concat_axis=0, tiled=True)
    ncol, rank = coeffs.shape[1], coeffs.shape[2]
    moved = moved.reshape(-1, u_bases.shape[0], ncol, rank, wide)
    residual, back = u_both(moved, u_bases, data)
    back = back.reshape(-1, ncol, rank, wide)
    back = lax.all_to_all(back, "col", split_axis=0, concat_axis=0, tiled=True)

    theirs = v_apply(tops, back, v_bases, 1, BF16)
    theirs = lax.ppermute(theirs, "row", swap)
    own = v_apply(tops, back, v_bases, 0, F32)
    met = (own + theirs.astype(F32)).reshape(chips, 2, wide, tile)
    total = met[0]
    for d in (2, 1, 3):
        total = total + lax.ppermute(met[d].astype(BF16), "row", hop(d)).astype(F32)
    gradient = total.reshape(2, 2, wide // 2, tile).transpose(0, 3, 1, 2)
    return residual.reshape(recorded.shape), gradient.reshape(wavefield.shape)


def solution(mesh):
    in_specs = (
        P(("col", "row"), None, None),
        P(("row", "col"), None, None),
        P("row", "col", None, None),
        P(("row", "col"), None, None, None),
        P("row", "col"),
    )
    out_specs = (P(("row", "col"), None, None), P(("col", "row"), None, None))
    step = functools.partial(body, mesh.shape["row"] // 2)
    return jax.shard_map(step, mesh=mesh, in_specs=in_specs, out_specs=out_specs, check_vma=False)
```

```python
import functools

import jax
import jax.numpy as jnp
from jax import lax
from jax.experimental import pallas as pl
from jax.experimental.pallas import tpu as pltpu
from jax.sharding import PartitionSpec as P

F32 = jnp.float32
BF16 = jnp.bfloat16
INSIDE = pl.BlockSpec(memory_space=pltpu.VMEM)


LAG = 22000
SMALL = pltpu.CompilerParams(vmem_limit_bytes=12 << 20)


def dot(a, b):
    return jnp.dot(a, b, preferred_element_type=F32)


def cost(flops, moved):
    return pl.CostEstimate(flops=flops, bytes_accessed=moved, transcendentals=0)


def column(away, flip, t, chips):
    me = lax.axis_index("row")
    core = lax.rem(me, 2)
    core = 1 - core if flip else core
    return lax.rem(lax.div(me, 2) + away, chips) * 4 + core * 2 + t


def v_adjoint_kernel(items, lag, ranks, v, *rest):
    out, mark = rest[-2:]
    tiles, ncol, twice, tile = v.shape
    rank = twice // 2
    half = ranks.shape[2]
    level = lax.broadcasted_iota(jnp.int32, (rank, half), 0)
    for (away, flip), x in zip(items, rest):
        for t in range(2):
            j = column(away, flip, t, ncol // 4)
            block = x[t]
            turned = jnp.concatenate([block[:, half:], -block[:, :half]], axis=1)
            real = v[:, j, :rank, :].reshape(tiles * rank, tile)
            imag = v[:, j, rank:, :].reshape(tiles * rank, tile)
            prod = dot(real, block) + dot(imag, turned)
            for i in range(tiles):
                keep = level < ranks[j, i : i + 1, :]
                piece = prod[i * rank : (i + 1) * rank]
                for part in (slice(0, half), slice(half, 2 * half)):
                    out[i, j, :, part] = jnp.where(keep, piece[:, part], 0.0).astype(BF16)
    mark[...] = jnp.zeros_like(mark)
    if lag:
        pl.when(lax.rem(lax.axis_index("row"), 2) == 1)(lambda: pl.delay(lag))


def v_adjoint(ranks, v, items, xs, held=(), lag=0):
    tiles, ncol, twice, tile = v.shape
    wide = xs[0].shape[2]
    more = tuple(held)
    work = 2 * len(xs) * tiles * twice * tile
    return pl.pallas_call(
        functools.partial(v_adjoint_kernel, items, lag),
        out_shape=(
            jax.ShapeDtypeStruct((tiles, ncol, twice // 2, wide), BF16),
            jax.ShapeDtypeStruct((8, 128), jnp.int32),
        ),
        in_specs=[INSIDE] * (2 + len(xs) + len(more)),
        out_specs=(INSIDE, INSIDE),
        input_output_aliases={2 + len(xs): 0} if more else {},
        cost_estimate=cost(2 * work * wide, 2 * work),
        compiler_params=SMALL,
        name="v_adjoint",
    )(ranks, v, *xs, *more)


def u_both_kernel(coeffs, u, recorded, residual, back):
    sources, rows, cols, rank, wide = coeffs.shape
    half = wide // 2
    tile = u.shape[3]

    def bases(i, s):
        real = u[i, s * cols : (s + 1) * cols, :rank, :].reshape(cols * rank, tile)
        imag = u[i, s * cols : (s + 1) * cols, rank:, :].reshape(cols * rank, tile)
        return real, imag

    for i in range(rows):
        total = jnp.zeros((wide, tile), F32)
        for s in range(sources):
            c = coeffs[s, i].reshape(cols * rank, wide).T
            turned = jnp.concatenate([-c[half:], c[:half]], axis=0)
            real, imag = bases(i, s)
            total = total + dot(c, real) + dot(turned, imag)
        res = total.T - recorded[i * tile : (i + 1) * tile, :].astype(F32)
        residual[i * tile : (i + 1) * tile, :] = res
        r = res.astype(BF16)
        turned = jnp.concatenate([r[:, half:], -r[:, :half]], axis=1)
        for s in range(sources):
            real, imag = bases(i, s)
            prod = dot(real, r) + dot(imag, turned)
            back[s, i] = prod.astype(BF16).reshape(cols, rank, wide)


def u_both(coeffs, u, recorded):
    rows, _, _, tile = u.shape
    wide = coeffs.shape[4]
    return pl.pallas_call(
        u_both_kernel,
        out_shape=(
            jax.ShapeDtypeStruct((rows * tile, wide), F32),
            jax.ShapeDtypeStruct(coeffs.shape, BF16),
        ),
        in_specs=[INSIDE] * 3,
        out_specs=(INSIDE, INSIDE),
        cost_estimate=cost(4 * u.size * wide, 2 * u.size),
        compiler_params=SMALL,
        name="u_both",
    )(coeffs, u, recorded)


def v_apply_kernel(away, ranks, back, v, out):
    tiles, ncol, twice, tile = v.shape
    rank = twice // 2
    half = back.shape[3] // 2
    level = lax.broadcasted_iota(jnp.int32, (rank, 2 * half), 0)
    for n in range(out.shape[0]):
        j = column(away, n // 2, n % 2, ncol // 4)
        rows = []
        for i in range(tiles):
            top = jnp.concatenate([ranks[j, i : i + 1, :]] * 2, axis=1)
            rows.append(jnp.where(level < top, back[i, j].astype(F32), 0.0))
        b = jnp.concatenate(rows, axis=0).astype(BF16).T
        turned = jnp.concatenate([-b[half:], b[:half]], axis=0)
        real = v[:, j, :rank, :].reshape(tiles * rank, tile)
        imag = v[:, j, rank:, :].reshape(tiles * rank, tile)
        out[n] = (dot(b, real) + dot(turned, imag)).astype(out.dtype)


def v_apply(ranks, back, v, away, dtype):
    tiles, _, twice, tile = v.shape
    wide = back.shape[3]
    work = 2 * 4 * tiles * twice * tile
    return pl.pallas_call(
        functools.partial(v_apply_kernel, away),
        out_shape=jax.ShapeDtypeStruct((4, wide, tile), dtype),
        in_specs=[INSIDE] * 3,
        out_specs=INSIDE,
        cost_estimate=cost(work * wide, work),
        compiler_params=SMALL,
        name="v_apply",
    )(ranks, back, v)


def body(chips, wavefield, recorded, v_bases, u_bases, ranks):
    tile = v_bases.shape[3]
    wide = 2 * wavefield.shape[2]
    swap = [(r, r ^ 1) for r in range(2 * chips)]
    away = range(1, chips)

    def hop(d):
        return [(r, (r + 2 * d) % (2 * chips)) for r in range(2 * chips)]

    mine = wavefield.reshape(-1, tile, wide)
    partner = lax.ppermute(mine, "row", swap)
    along = [lax.ppermute(mine, "row", hop(chips - d)) for d in away]
    tops = jnp.broadcast_to(ranks.T[:, :, None], ranks.shape[::-1] + (wide // 2,))
    data = recorded.reshape(-1, wide)
    coeffs, mark = v_adjoint(tops, v_bases, [(0, 0), (0, 1)], [mine, partner])
    mark, data = lax.optimization_barrier((mark, data))
    *along, mark = lax.optimization_barrier((*along, mark))
    others = [lax.ppermute(part, "row", swap) for part in along]
    coeffs, _ = v_adjoint(tops, v_bases, [(d, 0) for d in away], along, (coeffs, mark))
    coeffs, _ = v_adjoint(tops, v_bases, [(d, 1) for d in away], others, (coeffs,), LAG)

    moved = lax.all_to_all(coeffs, "col", split_axis=0, concat_axis=0, tiled=True)
    ncol, rank = coeffs.shape[1], coeffs.shape[2]
    moved = moved.reshape(-1, u_bases.shape[0], ncol, rank, wide)
    residual, back = u_both(moved, u_bases, data)
    back = back.reshape(-1, ncol, rank, wide)
    back = lax.all_to_all(back, "col", split_axis=0, concat_axis=0, tiled=True)

    moved = []
    for d in (2, 1, 3):
        moved.append(lax.ppermute(v_apply(tops, back, v_bases, d, BF16), "row", hop(d)))
    total = v_apply(tops, back, v_bases, 0, F32)
    for part in moved:
        total = total + part.astype(F32)
    total = total[:2] + lax.ppermute(total[2:].astype(BF16), "row", swap).astype(F32)
    gradient = total.reshape(2, 2, wide // 2, tile).transpose(0, 3, 1, 2)
    return residual.reshape(recorded.shape), gradient.reshape(wavefield.shape)


def solution(mesh):
    in_specs = (
        P(("col", "row"), None, None),
        P(("row", "col"), None, None),
        P("row", "col", None, None),
        P(("row", "col"), None, None, None),
        P("row", "col"),
    )
    out_specs = (P(("row", "col"), None, None), P(("col", "row"), None, None))
    step = functools.partial(body, mesh.shape["row"] // 2)
    return jax.shard_map(step, mesh=mesh, in_specs=in_specs, out_specs=out_specs, check_vma=False)
```
